32 devices in a mesh: row: 4 (over x, core), col: 8 (over z, y).
Axes of the slice: x: 2, y: 2, z: 4, core: 2. Of those that a mesh axis runs over, the one named last changes fastest.
Arguments:
- points: bfloat16 [65536, 256], P(('row', 'col')), may hold values from -6 to 6
- rotated_slot: int32 [65536], P(('row', 'col')), may hold values from 0 to 65535, as said below
- fine_attend_in: bfloat16 [2, 256, 768], replicated, may hold values from -8 to 8
- fine_attend_out: bfloat16 [2, 256, 256], replicated, may hold values from -0.375 to 0.375
- fine_gate_up: bfloat16 [2, 256, 2048], replicated, may hold values from -0.375 to 0.375
- fine_down: bfloat16 [2, 1024, 256], replicated, may hold values from -0.1875 to 0.1875
- pool_weight: bfloat16 [2048, 512], replicated, may hold values from -0.125 to 0.125
- coarse_attend_in: bfloat16 [512, 1536], replicated, may hold values from -8 to 8
- coarse_attend_out: bfloat16 [512, 512], replicated, may hold values from -0.25 to 0.25
- coarse_gate_up: bfloat16 [512, 4096], replicated, may hold values from -0.25 to 0.25
- coarse_down: bfloat16 [2048, 512], replicated, may hold values from -0.125 to 0.125
- unpool_weight: bfloat16 [512, 2048], replicated, may hold values from -0.25 to 0.25
Outputs:
- refined: bfloat16 [65536, 256], P(('row', 'col'))
The draws below stay inside these ranges and needn't reach their ends.
Inputs may be any that keep to these rules, and one draw needn't show every extreme that they name: rotated_slot is a permutation of all points; each point's rotated position lies on a device with the same col index; of the points of one device at most 1280 have rotated positions on any one device, and in every col group some device sends exactly 1280 to one device.
All inputs are finite; a program needn't handle non-finite values.
Results may differ from the reference program's by a relative error of at most 0.017.
Values may be sent and summed in bfloat16 or wider, within the bound.
A program may use at most 128 MiB of HBM per device.

```python
import math
import jax
import jax.numpy as jnp
from jax import lax

D = 256
HEADS = 8
FH = 1024
CW = 512
CHEADS = 8
CH = 2048
BALL = 256
PTS_DEV = 2048
POINTS = 65536
CBALL = 2048
CAP = 1280
N_ROW = 4
N_COL = 8


def draw_attend(key, model_width, leading):
    base = jnp.clip(jax.random.normal(key, (leading, model_width, 3, model_width), jnp.float32), -4.0, 4.0) / math.sqrt(model_width)
    query_part = base[:, :, 0]
    key_part = base[:, :, 1]
    value_part = base[:, :, 2]
    return jnp.concatenate((query_part, key_part, value_part), axis=-1)


def draw_fine_attend_in(key, part):
    return draw_attend(jax.random.fold_in(key, 11), D, 2).astype(jnp.bfloat16)


def draw_coarse_attend_in(key, part):
    return draw_attend(jax.random.fold_in(key, 13), CW, 1)[0].astype(jnp.bfloat16)


def draw_rotated_slot(key, part):
    key_order, key_shift, key_source, key_target = jax.random.split(jax.random.fold_in(key, 5), 4)
    orders = jax.vmap(lambda subkey: jax.random.permutation(subkey, N_ROW))(jax.random.split(key_order, N_COL))
    shifts = jax.random.randint(key_shift, (N_COL,), 1, N_ROW)
    source_rank = jax.vmap(lambda subkey: jnp.argsort(jax.random.permutation(subkey, PTS_DEV)))(jax.random.split(key_source, N_ROW * N_COL)).reshape(N_ROW, N_COL, PTS_DEV)
    target_spots = jax.vmap(lambda subkey: jax.random.permutation(subkey, PTS_DEV))(jax.random.split(key_target, N_ROW * N_COL)).reshape(N_ROW, N_COL, PTS_DEV)
    row_index = jnp.arange(N_ROW)[:, None]
    col_index = jnp.arange(N_COL)[None, :]
    first_target = orders[col_index, row_index]
    second = orders[col_index, (row_index + shifts[None, :]) % N_ROW]
    target = jnp.where(source_rank < CAP, first_target[:, :, None], second[:, :, None])
    local_spot = target_spots[target, col_index[:, :, None], source_rank]
    return ((target * N_COL + col_index[:, :, None]) * PTS_DEV + local_spot).reshape(-1).astype(jnp.int32)


def shard_levels(key, extent, shards, smallest, largest):
    def one(dim, parts):
        draws = jax.random.uniform(jax.random.fold_in(jax.random.fold_in(key, 6), dim), (parts,), jnp.float32, smallest / len(shards), largest / len(shards))
        return jnp.repeat(jnp.exp(draws), extent[dim] // parts).reshape((-1,) + (1,) * (len(extent) - dim - 1))

    gain = one(*shards[0])
    for cut in shards[1:]:
        gain = gain * one(*cut)
    return gain


def centred(rng, extent, scale, most, cuts=(), kind=jnp.bfloat16):
    drawn = scale * jax.random.normal(rng, extent, jnp.float32)
    if cuts:
        drawn = drawn * shard_levels(rng, extent, cuts, -0.22, 0.18)
    return jnp.clip(drawn, -most, most).astype(kind)


def setup_inputs(seed: int = 0) -> dict:
    key_list = jax.random.split(jax.random.key(seed), 13)
    return {
        "points": centred(key_list[0], (POINTS, D), 1.0, 6.0, ((0, 32),)),
        "rotated_slot": draw_rotated_slot(jax.random.fold_in(key_list[12], 71), 0),
        "fine_attend_in": draw_fine_attend_in(jax.random.fold_in(key_list[12], 71), 0),
        "fine_attend_out": centred(key_list[3], (2, D, D), D ** -0.5, 0.375),
        "fine_gate_up": centred(key_list[4], (2, D, 2 * FH), D ** -0.5, 0.375),
        "fine_down": centred(key_list[5], (2, FH, D), FH ** -0.5, 0.1875),
        "pool_weight": centred(key_list[6], (8 * D, CW), (8 * D) ** -0.5, 0.125),
        "coarse_attend_in": draw_coarse_attend_in(jax.random.fold_in(key_list[12], 71), 0),
        "coarse_attend_out": centred(key_list[8], (CW, CW), CW ** -0.5, 0.25),
        "coarse_gate_up": centred(key_list[9], (CW, 2 * CH), CW ** -0.5, 0.25),
        "coarse_down": centred(key_list[10], (CH, CW), CH ** -0.5, 0.125),
        "unpool_weight": centred(key_list[11], (CW, 8 * D), CW ** -0.5, 0.25),
    }


epsilon = 1e-06

def normed(source):
    widened = source.astype(jnp.float32)
    inverse_rms = lax.rsqrt(lax.optimization_barrier(jnp.mean(widened * widened, axis=-1, keepdims=True)) + epsilon)
    return (widened * inverse_rms).astype(jnp.bfloat16)

def ball_mix(queries, pairs, head_count):
    ball_count, query_len, model_width = queries.shape
    key_len = pairs.shape[1]
    head_size = model_width // head_count
    query_heads = queries.reshape(ball_count, query_len, head_count, head_size).astype(jnp.float32)
    key_heads = pairs[:, :, :model_width].reshape(ball_count, key_len, head_count, head_size).astype(jnp.float32)
    value_heads = pairs[:, :, model_width:].reshape(ball_count, key_len, head_count, head_size).astype(jnp.float32)
    scores = jnp.einsum('bqhd,bkhd->bhqk', query_heads, key_heads) * head_size ** (-0.5)
    row_max = lax.optimization_barrier(jnp.max(scores, axis=-1, keepdims=True))
    weights = jnp.exp(scores - row_max)
    weights = (weights / lax.optimization_barrier(jnp.sum(weights, axis=-1, keepdims=True))).astype(jnp.bfloat16)
    weights = lax.optimization_barrier(weights).astype(jnp.float32)
    mixture = jnp.einsum('bhqk,bkhd->bqhd', weights, value_heads)
    return mixture.reshape(ball_count, query_len, model_width).astype(jnp.bfloat16)

def attend(stream, attend_in, attend_out, head_count, ball_size):
    model_width = stream.shape[1]
    packed = jnp.dot(normed(stream), attend_in, preferred_element_type=jnp.float32).astype(jnp.bfloat16)
    queries = packed[:, :model_width].reshape(-1, ball_size, model_width)
    pairs = packed[:, model_width:].reshape(-1, ball_size, 2 * model_width)
    mixture = ball_mix(queries, pairs, head_count).reshape(-1, model_width)
    return jnp.dot(mixture, attend_out, preferred_element_type=jnp.float32)

def feed_forward(stream, gate_up, down_weight):
    both = jnp.dot(normed(stream), gate_up, preferred_element_type=jnp.float32)
    half_width = both.shape[1] // 2
    hidden = (jax.nn.silu(both[:, :half_width]) * both[:, half_width:]).astype(jnp.bfloat16)
    return (stream.astype(jnp.float32) + jnp.dot(hidden, down_weight, preferred_element_type=jnp.float32)).astype(jnp.bfloat16)

def blocked(function, source, block_size):
    pieces = source.reshape(-1, block_size, source.shape[-1])
    result = lax.map(function, pieces)
    return result.reshape(-1, result.shape[-1])

def reference(points, rotated_slot, fine_attend_in, fine_attend_out, fine_gate_up, fine_down, pool_weight, coarse_attend_in, coarse_attend_out, coarse_gate_up, coarse_down, unpool_weight):
    block_size = math.gcd(POINTS, 8192)

    def layer_one(stream):
        mixed = (stream.astype(jnp.float32) + attend(stream, fine_attend_in[0], fine_attend_out[0], HEADS, BALL)).astype(jnp.bfloat16)
        return feed_forward(mixed, fine_gate_up[0], fine_down[0])
    first = blocked(layer_one, points, block_size)
    rotated = jnp.zeros_like(first).at[rotated_slot].set(first)

    def turn(stream):
        return attend(stream, fine_attend_in[1], fine_attend_out[1], HEADS, BALL).astype(jnp.bfloat16)
    turned = blocked(turn, rotated, block_size)
    mixed_two = (first.astype(jnp.float32) + turned[rotated_slot].astype(jnp.float32)).astype(jnp.bfloat16)

    def layer_two(stream):
        return feed_forward(stream, fine_gate_up[1], fine_down[1])
    second = blocked(layer_two, mixed_two, block_size)
    pooled = jnp.dot(second.reshape(-1, 8 * D), pool_weight, preferred_element_type=jnp.float32).astype(jnp.bfloat16)

    def coarse_layer(stream):
        mixed = (stream.astype(jnp.float32) + attend(stream, coarse_attend_in, coarse_attend_out, CHEADS, CBALL)).astype(jnp.bfloat16)
        return feed_forward(mixed, coarse_gate_up, coarse_down)
    coarse = blocked(coarse_layer, pooled, CBALL)
    lifted = jnp.dot(normed(coarse), unpool_weight, preferred_element_type=jnp.float32).reshape(-1, D)
    return (second.astype(jnp.float32) + lifted).astype(jnp.bfloat16)
```

```python
import functools
import math

import jax
import jax.numpy as jnp
from jax import lax
from jax.experimental import pallas as pl
from jax.experimental.pallas import tpu as pltpu
from jax.sharding import PartitionSpec as P

HEADS = 8
CHEADS = 8
BALL = 256
GROUP = 8
FAN = 8
LANES = 128
EPS = 1e-06
F32 = jnp.float32
BF16 = jnp.bfloat16
LOG2E = 1.4426950408889634


def dot(a, b):
    return jnp.dot(a, b, preferred_element_type=F32)


def dot_t(a, b):
    return lax.dot_general(a, b, (((1,), (1,)), ((), ())), preferred_element_type=F32)


def normed(x):
    wide = x.astype(F32)
    return (wide * lax.rsqrt(jnp.mean(wide * wide, axis=-1, keepdims=True) + EPS)).astype(BF16)


def ff_sum(x, gate_up, down):
    both = dot(normed(x), gate_up)
    half = both.shape[1] // 2
    g = both[:, :half]
    hidden = ((0.5 * g) * (1.0 + jnp.tanh(0.5 * g)) * both[:, half:]).astype(BF16)
    return x.astype(F32) + dot(hidden, down)


def fine_attention(u, w_in, w_out):
    rows, width = u.shape
    packed = dot(normed(u), w_in).astype(BF16)
    q, k, v = packed[:, :width], packed[:, width:2 * width], packed[:, 2 * width:]
    size = width // HEADS
    factor = size ** -0.5 * LOG2E
    head_of = lax.broadcasted_iota(jnp.int32, (rows, width), 1) // size
    zero = jnp.zeros((), BF16)
    weights, values = [], []
    for h in range(HEADS):
        mine = head_of == h
        s = dot_t(jnp.where(mine, q, zero), k)
        m = jnp.max(s, axis=-1, keepdims=True)
        weights.append(jnp.exp2((s - m) * factor).astype(BF16))
        values.append(
            jnp.concatenate(
                (jnp.where(mine, v, zero), jnp.where(mine, jnp.ones((), BF16), zero)), axis=1
            )
        )
    both = dot(jnp.concatenate(weights, axis=1), jnp.concatenate(values, axis=0))
    mixture = (both[:, :width] / both[:, width:]).astype(BF16)
    return dot(mixture, w_out)


def row_peers():
    me = lax.axis_index("row")
    near = me + 1 - 2 * (me % 2)
    far = me + 2 - 4 * ((me // 2) % 2)
    return me, near, far


def greet(peers, axis):
    barrier = pltpu.get_barrier_semaphore()
    for peer in peers:
        pl.semaphore_signal(
            barrier, inc=1, device_id={axis: peer}, device_id_type=pl.DeviceIdType.MESH
        )
    pl.semaphore_wait(barrier, len(peers))


class RowGather:
    def __init__(self, out, chunk, send, recv):
        self.out, self.chunk, self.send, self.recv = out, chunk, send, recv
        self.me, self.near, self.far = row_peers()

    def copy(self, kind, c, block, peer):
        spot = self.out.at[block, pl.ds(c * self.chunk, self.chunk)]
        return pltpu.make_async_remote_copy(
            src_ref=spot,
            dst_ref=spot,
            send_sem=self.send.at[kind, c],
            recv_sem=self.recv.at[kind, c],
            device_id={"row": peer},
            device_id_type=pl.DeviceIdType.MESH,
        )

    def own(self, c):
        self.copy(0, c, self.me, self.far).start()
        self.copy(1, c, self.me, self.near).start()

    def relay(self, c):
        self.copy(0, c, self.far, self.far).wait_recv()
        self.copy(2, c, self.far, self.near).start()

    def finish(self, c):
        self.copy(0, c, self.me, self.far).wait_send()
        self.copy(1, c, self.me, self.near).wait_send()
        self.copy(2, c, self.far, self.near).wait_send()
        self.copy(1, c, self.near, self.near).wait_recv()
        self.copy(2, c, self.far + self.near - self.me, self.near).wait_recv()


LAG = 2


def layer_one_kernel(
    col_size, points, slots, w_in, w_out, gate_up, down, out, inverse, slot_all, send, recv,
    s_send, s_recv,
):
    rows = points.shape[0]
    count = rows // BALL
    me, near, far = row_peers()
    other = far + near - me
    greet((near, far, other), "row")
    slot_all[me] = slots[...]

    def slot_copy(kind, block, peer):
        return pltpu.make_async_remote_copy(
            src_ref=slots,
            dst_ref=slot_all.at[block],
            send_sem=s_send.at[kind],
            recv_sem=s_recv.at[kind],
            device_id={"row": peer},
            device_id_type=pl.DeviceIdType.MESH,
        )

    for kind, peer in enumerate((near, far, other)):
        slot_copy(kind, me, peer).start()
    gather = RowGather(out, BALL, send, recv)

    def step(b, carry):
        u = points[pl.ds(b * BALL, BALL), :]
        mixed = (u.astype(F32) + fine_attention(u, w_in[...], w_out[...])).astype(BF16)
        out[me, pl.ds(b * BALL, BALL), :] = ff_sum(mixed, gate_up[...], down[...]).astype(BF16)
        gather.own(b)

        @pl.when(b >= LAG)
        def _():
            gather.relay(b - LAG)

        return carry

    lax.fori_loop(0, count, step, 0)
    for kind, peer in enumerate((near, far, other)):
        slot_copy(kind, peer, peer).wait()
    lines, lanes = slots.shape
    row_id = lax.broadcasted_iota(jnp.int32, (lines, lanes), 0)
    lane_id = lax.broadcasted_iota(jnp.int32, (lines, lanes), 1).astype(F32)
    sub_id = lax.broadcasted_iota(jnp.int32, (lanes, lanes), 0)
    left, right = [], []
    for r in range(slot_all.shape[0]):
        for c in range(lines):
            line = slot_all[r, c:c + 1, :]
            line = jnp.where(line // (rows * col_size) == me, line % rows, rows)
            hit = row_id == line // lanes
            left.append(
                jnp.concatenate(
                    (jnp.where(hit, float(r * lines + c), 0.0), jnp.where(hit, lane_id, 0.0)),
                    axis=0,
                ).astype(BF16)
            )
            right.append(jnp.where(sub_id == line % lanes, 1.0, 0.0).astype(BF16))
    found = dot_t(jnp.concatenate(left, axis=1), jnp.concatenate(right, axis=1))
    inverse[...] = (found[:lines] * lanes + found[lines:]).astype(jnp.int32)

    def tail(c, carry):
        gather.relay(c)
        return carry

    lax.fori_loop(max(count - LAG, 0), count, tail, 0)

    def end(c, carry):
        gather.finish(c)
        return carry

    lax.fori_loop(0, count, end, 0)


def widen(source, wide):
    rows = source.shape[1]
    for block in range(source.shape[0]):

        def step(i, carry):
            at = pl.multiple_of(i * BALL, BALL)
            wide[pl.ds(block * rows + at, BALL), :] = source[
                block, pl.ds(at, BALL), :
            ].astype(F32)
            return carry

        lax.fori_loop(0, rows // BALL, step, 0)


def take_rows(wide, index, base, taken):
    unit = 32

    def step(i, carry):
        for j in range(unit):
            at = i * unit + j
            taken[pl.ds(at, 1), :] = wide[pl.ds(index[base + at], 1), :]
        return carry

    lax.fori_loop(0, taken.shape[0] // unit, step, 0)


def turn_kernel(first, index, w_in, w_out, out, wide, taken, send, recv):
    rows = first.shape[1]
    count = rows // BALL
    me, near, far = row_peers()
    greet((near, far), "row")
    gather = RowGather(out, BALL, send, recv)
    widen(first, wide)

    def step(b, carry):
        take_rows(wide, index, b * BALL, taken)
        u = taken[...].astype(BF16)
        out[me, pl.ds(b * BALL, BALL), :] = fine_attention(u, w_in[...], w_out[...]).astype(BF16)
        gather.own(b)

        @pl.when(b >= LAG)
        def _():
            gather.relay(b - LAG)

        return carry

    lax.fori_loop(0, count, step, 0)

    def tail(c, carry):
        gather.relay(c)
        return carry

    lax.fori_loop(max(count - LAG, 0), count, tail, 0)

    def end(c, carry):
        gather.finish(c)
        return carry

    lax.fori_loop(0, count, end, 0)


def layer_two_kernel(
    first, turned, index, gate_up, down, pool, second, pooled, wide, taken, tall, send, recv
):
    rows = second.shape[0]
    count = rows // BALL
    small = BALL // FAN
    col = lax.axis_index("col")
    me = col % GROUP
    base = col - me
    me_row = lax.axis_index("row")
    flip = me + 1 - 2 * (me % 2)
    peers = [(me + 2 * step) % GROUP for step in range(1, GROUP // 2)]
    greet([base + p for p in [flip] + peers], "col")
    widen(turned, wide)
    pieces = recv.shape[1]
    piece = pooled.shape[1] // pieces
    per = count // pieces

    def copy(kind, c, block, peer):
        spot = pooled.at[block, pl.ds(c * piece, piece)]
        return pltpu.make_async_remote_copy(
            src_ref=spot,
            dst_ref=spot,
            send_sem=send.at[kind, c],
            recv_sem=recv.at[kind, c],
            device_id={"col": base + peer},
            device_id_type=pl.DeviceIdType.MESH,
        )

    lead = GROUP // 2

    def source_of(kind):
        return (me + GROUP - 2 * kind) % GROUP

    def step(c, carry):
        def ball(i, carry):
            b = c * per + i
            at = pl.multiple_of(b * BALL, BALL)
            take_rows(wide, index, b * BALL, taken)
            mixed = (
                first[me_row, pl.ds(at, BALL), :].astype(F32) + taken[...]
            ).astype(BF16)
            result = ff_sum(mixed, gate_up[...], down[...]).astype(BF16)
            second[pl.ds(at, BALL), :] = result
            for t in range(tall.shape[0]):
                tall[t, pl.ds(pl.multiple_of(i * BALL, BALL), BALL), :] = result[
                    :, t * LANES:(t + 1) * LANES
                ].astype(F32)
            return carry

        lax.fori_loop(0, per, ball, 0)
        side = [
            tall[t, pl.ds(j, piece, stride=FAN), :].astype(BF16)
            for j in range(FAN)
            for t in range(tall.shape[0])
        ]
        total = dot(jnp.concatenate(side, axis=1), pool[...])
        pooled[me, pl.ds(pl.multiple_of(c * piece, piece), piece), :] = total.astype(BF16)
        copy(0, c, me, flip).start()
        for kind in range(1, lead):
            copy(kind, c, me, peers[kind - 1]).start()
        return carry

    lax.fori_loop(0, pieces, step, 0)

    def relay(c, carry):
        for kind in range(1, lead):
            copy(kind, c, source_of(kind), peers[0]).wait_recv()
            copy(lead - 1 + kind, c, source_of(kind), flip).start()
        return carry

    lax.fori_loop(0, pieces, relay, 0)

    def end(c, carry):
        copy(0, c, me, flip).wait_send()
        copy(0, c, flip, flip).wait_recv()
        for kind in range(1, lead):
            copy(kind, c, me, peers[kind - 1]).wait_send()
            copy(lead - 1 + kind, c, source_of(kind), flip).wait_send()
            origin = source_of(kind)
            copy(lead - 1 + kind, c, origin + 1 - 2 * (origin % 2), flip).wait_recv()
        return carry

    lax.fori_loop(0, pieces, end, 0)


def coarse_kernel(
    pooled, second, w_in, w_out, gate_up, down, unpool, out, keys, values, lifted
):
    me = lax.axis_index("col") % GROUP
    own = pooled[me]
    rows, width = own.shape
    size = width // CHEADS
    factor = size ** -0.5 * LOG2E
    for block in range(GROUP):
        packed = dot(normed(pooled[block]), w_in[:, width:]).astype(BF16)
        keys[pl.ds(block * rows, rows), :] = packed[:, :width]
        values[pl.ds(block * rows, rows), :] = packed[:, width:]
    q = dot(normed(own), w_in[:, :width]).astype(BF16)
    part = 256
    head_of = lax.broadcasted_iota(jnp.int32, (rows, part), 1) // size
    zero = jnp.zeros((), BF16)
    mixture = []
    for g in range(width // part):
        at = g * part
        acc = jnp.zeros((rows, part), F32)
        for h in range(part // size):
            mine = head_of == h
            s = dot_t(jnp.where(mine, q[:, at:at + part], zero), keys[:, at:at + part])
            m = jnp.max(s, axis=-1, keepdims=True)
            e = jnp.exp2((s - m) * factor)
            r = dot(e.astype(BF16), values[:, at:at + part])
            acc = jnp.where(mine, r / jnp.sum(e, axis=-1, keepdims=True), acc)
        mixture.append(acc.astype(BF16))
    mixed = (own.astype(F32) + dot(jnp.concatenate(mixture, axis=1), w_out[...])).astype(BF16)
    coarse = ff_sum(mixed, gate_up[...], down[...]).astype(BF16)
    up = normed(coarse)
    fine = out.shape[1]
    for j in range(FAN):
        part_up = dot(up, unpool[:, j * fine:(j + 1) * fine])
        for t in range(lifted.shape[0]):
            lifted[t, pl.ds(j, rows, stride=FAN), :] = part_up[:, t * LANES:(t + 1) * LANES]
    for c in range(out.shape[0] // BALL):
        at = c * BALL
        for t in range(lifted.shape[0]):
            lane = slice(t * LANES, (t + 1) * LANES)
            out[at:at + BALL, lane] = (
                second[at:at + BALL, lane].astype(F32) + lifted[t, at:at + BALL, :]
            ).astype(BF16)


VMEM = pl.BlockSpec(memory_space=pltpu.VMEM)
SMEM = pl.BlockSpec(memory_space=pltpu.SMEM)
DMA = pltpu.SemaphoreType.DMA


def local(
    points,
    rotated_slot,
    fine_attend_in,
    fine_attend_out,
    fine_gate_up,
    fine_down,
    pool_weight,
    coarse_attend_in,
    coarse_attend_out,
    coarse_gate_up,
    coarse_down,
    unpool_weight,
):
    rows, width = points.shape
    row_size = lax.axis_size("row")
    col_size = lax.axis_size("col")
    count = rows // BALL
    small = rows // FAN
    coarse_width = pool_weight.shape[1]
    lanes = LANES
    lines = rows // lanes
    grant = 48 * 1024 * 1024
    everyone = jax.ShapeDtypeStruct((row_size, rows, width), BF16)

    first, inverse = pl.pallas_call(
        functools.partial(layer_one_kernel, col_size),
        out_shape=(everyone, jax.ShapeDtypeStruct((lines, lanes), jnp.int32)),
        in_specs=[VMEM] * 6,
        out_specs=(VMEM, VMEM),
        scratch_shapes=[
            pltpu.VMEM((row_size, lines, lanes), jnp.int32),
            DMA((3, count)),
            DMA((3, count)),
            DMA((3,)),
            DMA((3,)),
        ],
        compiler_params=pltpu.CompilerParams(
            collective_id=0, has_side_effects=True, vmem_limit_bytes=grant
        ),
        name="layer_one",
    )(
        points,
        rotated_slot.reshape(lines, lanes),
        fine_attend_in[0],
        fine_attend_out[0],
        fine_gate_up[0],
        fine_down[0],
    )

    turned = pl.pallas_call(
        turn_kernel,
        out_shape=everyone,
        in_specs=[VMEM, SMEM, VMEM, VMEM],
        out_specs=VMEM,
        scratch_shapes=[
            pltpu.VMEM((row_size * rows, width), F32),
            pltpu.VMEM((BALL, width), F32),
            DMA((3, count)),
            DMA((3, count)),
        ],
        compiler_params=pltpu.CompilerParams(
            collective_id=1, has_side_effects=True, vmem_limit_bytes=grant
        ),
        name="turn",
    )(first, inverse.reshape(-1), fine_attend_in[1], fine_attend_out[1])

    target = rotated_slot // (rows * col_size)
    index = target * rows + rotated_slot % rows
    pieces = 2
    kinds = GROUP - 1
    second, pooled = pl.pallas_call(
        layer_two_kernel,
        out_shape=(
            jax.ShapeDtypeStruct((rows, width), BF16),
            jax.ShapeDtypeStruct((GROUP, small, coarse_width), BF16),
        ),
        in_specs=[VMEM, VMEM, SMEM, VMEM, VMEM, VMEM],
        out_specs=(VMEM, VMEM),
        scratch_shapes=[
            pltpu.VMEM((row_size * rows, width), F32),
            pltpu.VMEM((BALL, width), F32),
            pltpu.VMEM((width // LANES, rows // pieces, LANES), F32),
            DMA((kinds, pieces)),
            DMA((kinds, pieces)),
        ],
        compiler_params=pltpu.CompilerParams(
            collective_id=2, has_side_effects=True, vmem_limit_bytes=grant
        ),
        name="layer_two",
    )(first, turned, index, fine_gate_up[1], fine_down[1], pool_weight)

    return pl.pallas_call(
        coarse_kernel,
        out_shape=jax.ShapeDtypeStruct((rows, width), BF16),
        in_specs=[VMEM] * 7,
        out_specs=VMEM,
        scratch_shapes=[
            pltpu.VMEM((GROUP * small, coarse_width), BF16),
            pltpu.VMEM((GROUP * small, coarse_width), BF16),
            pltpu.VMEM((width // LANES, rows, LANES), F32),
        ],
        compiler_params=pltpu.CompilerParams(vmem_limit_bytes=grant),
        name="coarse",
    )(
        pooled,
        second,
        coarse_attend_in,
        coarse_attend_out,
        coarse_gate_up,
        coarse_down,
        unpool_weight,
    )


def solution(mesh):
    split = P(("row", "col"), None)
    placed = (split, P(("row", "col"))) + (P(),) * 10
    return jax.shard_map(local, mesh=mesh, in_specs=placed, out_specs=split, check_vma=False)
```

```python
import functools
import math

import jax
import jax.numpy as jnp
from jax import lax
from jax.experimental import pallas as pl
from jax.experimental.pallas import tpu as pltpu
from jax.sharding import PartitionSpec as P

HEADS = 8
CHEADS = 8
BALL = 256
GROUP = 8
FAN = 8
LANES = 128
EPS = 1e-06
F32 = jnp.float32
BF16 = jnp.bfloat16
LOG2E = 1.4426950408889634


def dot(a, b):
    return jnp.dot(a, b, preferred_element_type=F32)


def dot_t(a, b):
    return lax.dot_general(a, b, (((1,), (1,)), ((), ())), preferred_element_type=F32)


def normed(x):
    wide = x.astype(F32)
    return (wide * lax.rsqrt(jnp.mean(wide * wide, axis=-1, keepdims=True) + EPS)).astype(BF16)


def ff_sum(x, gate_up, down):
    both = dot(normed(x), gate_up)
    half = both.shape[1] // 2
    g = both[:, :half]
    hidden = ((0.5 * g) * (1.0 + jnp.tanh(0.5 * g)) * both[:, half:]).astype(BF16)
    return x.astype(F32) + dot(hidden, down)


def fine_attention(u, w_in, w_out):
    rows, width = u.shape
    packed = dot(normed(u), w_in).astype(BF16)
    q, k, v = packed[:, :width], packed[:, width:2 * width], packed[:, 2 * width:]
    size = width // HEADS
    factor = size ** -0.5 * LOG2E
    head_of = lax.broadcasted_iota(jnp.int32, (rows, width), 1) // size
    zero = jnp.zeros((), BF16)
    weights, values = [], []
    for h in range(HEADS):
        mine = head_of == h
        s = dot_t(jnp.where(mine, q, zero), k)
        m = jnp.max(s, axis=-1, keepdims=True)
        weights.append(jnp.exp2((s - m) * factor).astype(BF16))
        values.append(
            jnp.concatenate(
                (jnp.where(mine, v, zero), jnp.where(mine, jnp.ones((), BF16), zero)), axis=1
            )
        )
    both = dot(jnp.concatenate(weights, axis=1), jnp.concatenate(values, axis=0))
    mixture = (both[:, :width] / both[:, width:]).astype(BF16)
    return dot(mixture, w_out)


def row_peers():
    me = lax.axis_index("row")
    near = me + 1 - 2 * (me % 2)
    far = me + 2 - 4 * ((me // 2) % 2)
    return me, near, far


def greet(peers, axis):
    barrier = pltpu.get_barrier_semaphore()
    for peer in peers:
        pl.semaphore_signal(
            barrier, inc=1, device_id={axis: peer}, device_id_type=pl.DeviceIdType.MESH
        )
    pl.semaphore_wait(barrier, len(peers))


class RowGather:
    def __init__(self, held, wide, chunk, send, recv):
        self.held, self.wide, self.chunk = held, wide, chunk
        self.send, self.recv = send, recv
        self.me, self.near, self.far = row_peers()
        self.last = self.far + self.near - self.me

    def copy(self, kind, c, block, peer):
        spot = self.held.at[block, pl.ds(c * self.chunk, self.chunk)]
        return pltpu.make_async_remote_copy(
            src_ref=spot,
            dst_ref=spot,
            send_sem=self.send.at[kind, c],
            recv_sem=self.recv.at[kind, c],
            device_id={"row": peer},
            device_id_type=pl.DeviceIdType.MESH,
        )

    def widen(self, block, c):
        rows = self.held.shape[1]
        at = pl.multiple_of(block * rows + c * self.chunk, self.chunk)
        self.wide[pl.ds(at, self.chunk), :] = self.held[
            block, pl.ds(pl.multiple_of(c * self.chunk, self.chunk), self.chunk), :
        ].astype(F32)

    def own(self, c, value):
        at = pl.multiple_of(c * self.chunk, self.chunk)
        self.held[self.me, pl.ds(at, self.chunk), :] = value
        self.copy(0, c, self.me, self.far).start()
        self.copy(1, c, self.me, self.near).start()
        self.widen(self.me, c)

    def relay(self, c):
        self.copy(0, c, self.far, self.far).wait_recv()
        self.copy(2, c, self.far, self.near).start()
        self.widen(self.far, c)
        self.copy(1, c, self.near, self.near).wait_recv()
        self.widen(self.near, c)

    def arrive(self, c):
        self.copy(2, c, self.last, self.near).wait_recv()
        self.widen(self.last, c)

    def inside(self, b):
        @pl.when(b >= LAG)
        def _():
            self.relay(b - LAG)

        @pl.when(b >= LAG + 1)
        def _():
            self.arrive(b - LAG - 1)

    def finish(self, count):
        def tail(c, carry):
            self.relay(c)

            @pl.when(c >= 1)
            def _():
                self.arrive(c - 1)

            return carry

        lax.fori_loop(max(count - LAG, 0), count, tail, 0)
        self.arrive(count - 1)

        def end(c, carry):
            self.copy(0, c, self.me, self.far).wait_send()
            self.copy(1, c, self.me, self.near).wait_send()
            self.copy(2, c, self.far, self.near).wait_send()
            return carry

        lax.fori_loop(0, count, end, 0)


LAG = 2
COL_LAG = 3


def layer_one_kernel(
    col_size, points, slots, w_in, w_out, gate_up, down, out, wide, inverse, route, held,
    slot_all, send, recv, s_send, s_recv,
):
    rows = points.shape[0]
    count = rows // BALL
    me, near, far = row_peers()
    other = far + near - me
    greet((near, far, other), "row")
    slot_all[me] = slots[...]

    def slot_copy(kind, block, peer):
        return pltpu.make_async_remote_copy(
            src_ref=slots,
            dst_ref=slot_all.at[block],
            send_sem=s_send.at[kind],
            recv_sem=s_recv.at[kind],
            device_id={"row": peer},
            device_id_type=pl.DeviceIdType.MESH,
        )

    for kind, peer in enumerate((near, far, other)):
        slot_copy(kind, me, peer).start()
    route[...] = slots[...] // (rows * col_size) * rows + slots[...] % rows
    gather = RowGather(held, wide, BALL, send, recv)

    def step(b, carry):
        u = points[pl.ds(b * BALL, BALL), :]
        mixed = (u.astype(F32) + fine_attention(u, w_in[0], w_out[0])).astype(BF16)
        value = ff_sum(mixed, gate_up[0], down[0]).astype(BF16)
        out[pl.ds(pl.multiple_of(b * BALL, BALL), BALL), :] = value
        gather.own(b, value)
        gather.inside(b)
        return carry

    lax.fori_loop(0, count, step, 0)
    for kind, peer in enumerate((near, far, other)):
        slot_copy(kind, peer, peer).wait()
    lines, lanes = slots.shape
    row_id = lax.broadcasted_iota(jnp.int32, (lines, lanes), 0)
    lane_id = lax.broadcasted_iota(jnp.int32, (lines, lanes), 1).astype(F32)
    sub_id = lax.broadcasted_iota(jnp.int32, (lanes, lanes), 0)
    left, right = [], []
    for r in range(slot_all.shape[0]):
        for c in range(lines):
            line = slot_all[r, c:c + 1, :]
            line = jnp.where(line // (rows * col_size) == me, line % rows, rows)
            hit = row_id == line // lanes
            left.append(
                jnp.concatenate(
                    (jnp.where(hit, float(r * lines + c), 0.0), jnp.where(hit, lane_id, 0.0)),
                    axis=0,
                ).astype(BF16)
            )
            right.append(jnp.where(sub_id == line % lanes, 1.0, 0.0).astype(BF16))
    found = dot_t(jnp.concatenate(left, axis=1), jnp.concatenate(right, axis=1))
    inverse[...] = (found[:lines] * lanes + found[lines:]).astype(jnp.int32)

    gather.finish(count)


def take_rows(wide, index, base, taken):
    unit = 32

    def step(i, carry):
        for j in range(unit):
            at = i * unit + j
            taken[pl.ds(at, 1), :] = wide[pl.ds(index[base + at], 1), :]
        return carry

    lax.fori_loop(0, taken.shape[0] // unit, step, 0)


def turn_kernel(source, index, w_in, w_out, wide, held, taken, send, recv):
    rows = held.shape[1]
    count = rows // BALL
    me, near, far = row_peers()
    greet((near, far), "row")
    gather = RowGather(held, wide, BALL, send, recv)

    def step(b, carry):
        take_rows(source, index, b * BALL, taken)
        u = taken[...].astype(BF16)
        gather.own(b, fine_attention(u, w_in[1], w_out[1]).astype(BF16))
        gather.inside(b)
        return carry

    lax.fori_loop(0, count, step, 0)

    gather.finish(count)


def layer_two_kernel(
    first, wide, index, gate_up, down, pool, second, pooled, taken, tall, send, recv
):
    rows = second.shape[0]
    count = rows // BALL
    small = BALL // FAN
    col = lax.axis_index("col")
    me = col % GROUP
    base = col - me
    flip = me + 1 - 2 * (me % 2)
    peers = [(me + 2 * step) % GROUP for step in range(1, GROUP // 2)]
    greet([base + p for p in [flip] + peers], "col")
    pieces = recv.shape[1]
    piece = pooled.shape[1] // pieces
    per = count // pieces

    def copy(kind, c, block, peer):
        spot = pooled.at[block, pl.ds(c * piece, piece)]
        return pltpu.make_async_remote_copy(
            src_ref=spot,
            dst_ref=spot,
            send_sem=send.at[kind, c],
            recv_sem=recv.at[kind, c],
            device_id={"col": base + peer},
            device_id_type=pl.DeviceIdType.MESH,
        )

    lead = GROUP // 2

    def source_of(kind):
        return (me + GROUP - 2 * kind) % GROUP

    def step(c, carry):
        def ball(i, carry):
            b = c * per + i
            at = pl.multiple_of(b * BALL, BALL)
            take_rows(wide, index, b * BALL, taken)
            mixed = (
                first[pl.ds(at, BALL), :].astype(F32) + taken[...]
            ).astype(BF16)
            result = ff_sum(mixed, gate_up[1], down[1]).astype(BF16)
            second[pl.ds(at, BALL), :] = result
            for t in range(tall.shape[0]):
                tall[t, pl.ds(pl.multiple_of(i * BALL, BALL), BALL), :] = result[
                    :, t * LANES:(t + 1) * LANES
                ].astype(F32)
            return carry

        lax.fori_loop(0, per, ball, 0)
        side = [
            tall[t, pl.ds(j, piece, stride=FAN), :].astype(BF16)
            for j in range(FAN)
            for t in range(tall.shape[0])
        ]
        total = dot(jnp.concatenate(side, axis=1), pool[...])
        pooled[me, pl.ds(pl.multiple_of(c * piece, piece), piece), :] = total.astype(BF16)
        copy(0, c, me, flip).start()
        for kind in range(1, lead):
            copy(kind, c, me, peers[kind - 1]).start()

        @pl.when(c >= COL_LAG)
        def _():
            relay(c - COL_LAG, 0)

        return carry

    def relay(c, carry):
        for kind in range(1, lead):
            copy(kind, c, source_of(kind), peers[0]).wait_recv()
            copy(lead - 1 + kind, c, source_of(kind), flip).start()
        return carry

    lax.fori_loop(0, pieces, step, 0)
    lax.fori_loop(max(pieces - COL_LAG, 0), pieces, relay, 0)

    def end(c, carry):
        copy(0, c, me, flip).wait_send()
        copy(0, c, flip, flip).wait_recv()
        for kind in range(1, lead):
            copy(kind, c, me, peers[kind - 1]).wait_send()
            copy(lead - 1 + kind, c, source_of(kind), flip).wait_send()
            origin = source_of(kind)
            copy(lead - 1 + kind, c, origin + 1 - 2 * (origin % 2), flip).wait_recv()
        return carry

    lax.fori_loop(0, pieces, end, 0)


def coarse_kernel(
    pooled, second, w_in, w_out, gate_up, down, unpool, out, keys, values, lifted
):
    me = lax.axis_index("col") % GROUP
    own = pooled[me]
    rows, width = own.shape
    size = width // CHEADS
    factor = size ** -0.5 * LOG2E
    for block in range(GROUP):
        packed = dot(normed(pooled[block]), w_in[:, width:]).astype(BF16)
        keys[pl.ds(block * rows, rows), :] = packed[:, :width]
        values[pl.ds(block * rows, rows), :] = packed[:, width:]
    q = dot(normed(own), w_in[:, :width]).astype(BF16)
    part = 256
    head_of = lax.broadcasted_iota(jnp.int32, (rows, part), 1) // size
    zero = jnp.zeros((), BF16)
    mixture = []
    for g in range(width // part):
        at = g * part
        acc = jnp.zeros((rows, part), F32)
        for h in range(part // size):
            mine = head_of == h
            s = dot_t(jnp.where(mine, q[:, at:at + part], zero), keys[:, at:at + part])
            m = jnp.max(s, axis=-1, keepdims=True)
            e = jnp.exp2((s - m) * factor)
            r = dot(e.astype(BF16), values[:, at:at + part])
            acc = jnp.where(mine, r / jnp.sum(e, axis=-1, keepdims=True), acc)
        mixture.append(acc.astype(BF16))
    mixed = (own.astype(F32) + dot(jnp.concatenate(mixture, axis=1), w_out[...])).astype(BF16)
    coarse = ff_sum(mixed, gate_up[...], down[...]).astype(BF16)
    up = normed(coarse)
    fine = out.shape[1]
    for j in range(FAN):
        part_up = dot(up, unpool[:, j * fine:(j + 1) * fine])
        for t in range(lifted.shape[0]):
            lifted[t, pl.ds(j, rows, stride=FAN), :] = part_up[:, t * LANES:(t + 1) * LANES]
    for c in range(out.shape[0] // BALL):
        at = c * BALL
        for t in range(lifted.shape[0]):
            lane = slice(t * LANES, (t + 1) * LANES)
            out[at:at + BALL, lane] = (
                second[at:at + BALL, lane].astype(F32) + lifted[t, at:at + BALL, :]
            ).astype(BF16)


VMEM = pl.BlockSpec(memory_space=pltpu.VMEM)
SMEM = pl.BlockSpec(memory_space=pltpu.SMEM)
DMA = pltpu.SemaphoreType.DMA


def local(
    points,
    rotated_slot,
    fine_attend_in,
    fine_attend_out,
    fine_gate_up,
    fine_down,
    pool_weight,
    coarse_attend_in,
    coarse_attend_out,
    coarse_gate_up,
    coarse_down,
    unpool_weight,
):
    rows, width = points.shape
    row_size = lax.axis_size("row")
    col_size = lax.axis_size("col")
    count = rows // BALL
    small = rows // FAN
    coarse_width = pool_weight.shape[1]
    lanes = LANES
    lines = rows // lanes
    mib = 1024 * 1024
    everyone = jax.ShapeDtypeStruct((row_size * rows, width), F32)
    held = pltpu.VMEM((row_size, rows, width), BF16)
    scalars = jax.ShapeDtypeStruct((lines, lanes), jnp.int32)

    first, wide, inverse, route = pl.pallas_call(
        functools.partial(layer_one_kernel, col_size),
        out_shape=(jax.ShapeDtypeStruct((rows, width), BF16), everyone, scalars, scalars),
        in_specs=[
            VMEM,
            VMEM,
            VMEM,
            VMEM,
            VMEM,
            VMEM,
        ],
        out_specs=(VMEM,) * 4,
        scratch_shapes=[
            held,
            pltpu.VMEM((row_size, lines, lanes), jnp.int32),
            DMA((3, count)),
            DMA((3, count)),
            DMA((3,)),
            DMA((3,)),
        ],
        compiler_params=pltpu.CompilerParams(
            collective_id=0, has_side_effects=True, vmem_limit_bytes=36 * mib
        ),
        name="layer_one",
    )(
        points,
        rotated_slot.reshape(lines, lanes),
        fine_attend_in,
        fine_attend_out,
        fine_gate_up,
        fine_down,
    )

    turned = pl.pallas_call(
        turn_kernel,
        out_shape=everyone,
        in_specs=[VMEM, SMEM, VMEM, VMEM],
        out_specs=VMEM,
        scratch_shapes=[
            held,
            pltpu.VMEM((BALL, width), F32),
            DMA((3, count)),
            DMA((3, count)),
        ],
        compiler_params=pltpu.CompilerParams(
            collective_id=1, has_side_effects=True, vmem_limit_bytes=32 * mib
        ),
        name="turn",
    )(wide, inverse.reshape(-1), fine_attend_in, fine_attend_out)

    pieces = count
    kinds = GROUP - 1
    second, pooled = pl.pallas_call(
        layer_two_kernel,
        out_shape=(
            jax.ShapeDtypeStruct((rows, width), BF16),
            jax.ShapeDtypeStruct((GROUP, small, coarse_width), BF16),
        ),
        in_specs=[VMEM, VMEM, SMEM, VMEM, VMEM, VMEM],
        out_specs=(VMEM, VMEM),
        scratch_shapes=[
            pltpu.VMEM((BALL, width), F32),
            pltpu.VMEM((width // LANES, rows // pieces, LANES), F32),
            DMA((kinds, pieces)),
            DMA((kinds, pieces)),
        ],
        compiler_params=pltpu.CompilerParams(
            collective_id=2, has_side_effects=True, vmem_limit_bytes=28 * mib
        ),
        name="layer_two",
    )(first, turned, route.reshape(-1), fine_gate_up, fine_down, pool_weight)

    return pl.pallas_call(
        coarse_kernel,
        out_shape=jax.ShapeDtypeStruct((rows, width), BF16),
        in_specs=[VMEM] * 7,
        out_specs=VMEM,
        scratch_shapes=[
            pltpu.VMEM((GROUP * small, coarse_width), BF16),
            pltpu.VMEM((GROUP * small, coarse_width), BF16),
            pltpu.VMEM((width // LANES, rows, LANES), F32),
        ],
        compiler_params=pltpu.CompilerParams(vmem_limit_bytes=36 * mib),
        name="coarse",
    )(
        pooled,
        second,
        coarse_attend_in,
        coarse_attend_out,
        coarse_gate_up,
        coarse_down,
        unpool_weight,
    )


def solution(mesh):
    split = P(("row", "col"), None)
    placed = (split, P(("row", "col"))) + (P(),) * 10
    return jax.shard_map(local, mesh=mesh, in_specs=placed, out_specs=split, check_vma=False)
```

```python
import functools
import math

import jax
import jax.numpy as jnp
from jax import lax
from jax.experimental import pallas as pl
from jax.experimental.pallas import tpu as pltpu
from jax.sharding import PartitionSpec as P

HEADS = 8
CHEADS = 8
BALL = 256
GROUP = 8
FAN = 8
LANES = 128
EPS = 1e-06
F32 = jnp.float32
BF16 = jnp.bfloat16
LOG2E = 1.4426950408889634


def dot(a, b):
    return jnp.dot(a, b, preferred_element_type=F32)


def dot_t(a, b):
    return lax.dot_general(a, b, (((1,), (1,)), ((), ())), preferred_element_type=F32)


def normed(x):
    wide = x.astype(F32)
    return (wide * lax.rsqrt(jnp.mean(wide * wide, axis=-1, keepdims=True) + EPS)).astype(BF16)


def ff_sum(x, gate_up, down):
    both = dot(normed(x), gate_up)
    half = both.shape[1] // 2
    g = both[:, :half]
    hidden = ((0.5 * g) * (1.0 + jnp.tanh(0.5 * g)) * both[:, half:]).astype(BF16)
    return x.astype(F32) + dot(hidden, down)


def fine_attention(u, w_in, w_out):
    rows, width = u.shape
    packed = dot(normed(u), w_in).astype(BF16)
    q, k, v = packed[:, :width], packed[:, width:2 * width], packed[:, 2 * width:]
    size = width // HEADS
    factor = size ** -0.5 * LOG2E
    head_of = lax.broadcasted_iota(jnp.int32, (rows, width), 1) // size
    zero = jnp.zeros((), BF16)
    weights, values = [], []
    for h in range(HEADS):
        mine = head_of == h
        s = dot_t(jnp.where(mine, q, zero), k)
        m = jnp.max(s, axis=-1, keepdims=True)
        weights.append(jnp.exp2((s - m) * factor).astype(BF16))
        values.append(
            jnp.concatenate(
                (jnp.where(mine, v, zero), jnp.where(mine, jnp.ones((), BF16), zero)), axis=1
            )
        )
    both = dot(jnp.concatenate(weights, axis=1), jnp.concatenate(values, axis=0))
    mixture = (both[:, :width] / both[:, width:]).astype(BF16)
    return dot(mixture, w_out)


def row_peers():
    me = lax.axis_index("row")
    near = me + 1 - 2 * (me % 2)
    far = me + 2 - 4 * ((me // 2) % 2)
    return me, near, far


def greet(peers, axis):
    barrier = pltpu.get_barrier_semaphore()
    for peer in peers:
        pl.semaphore_signal(
            barrier, inc=1, device_id={axis: peer}, device_id_type=pl.DeviceIdType.MESH
        )
    pl.semaphore_wait(barrier, len(peers))


class RowGather:
    def __init__(self, held, wide, chunk, send, recv):
        self.held, self.wide, self.chunk = held, wide, chunk
        self.send, self.recv = send, recv
        self.me, self.near, self.far = row_peers()
        self.last = self.far + self.near - self.me

    def copy(self, kind, c, block, peer):
        spot = self.held.at[block, pl.ds(c * self.chunk, self.chunk)]
        return pltpu.make_async_remote_copy(
            src_ref=spot,
            dst_ref=spot,
            send_sem=self.send.at[kind, c],
            recv_sem=self.recv.at[kind, c],
            device_id={"row": peer},
            device_id_type=pl.DeviceIdType.MESH,
        )

    def widen(self, block, c):
        rows = self.held.shape[1]
        at = pl.multiple_of(block * rows + c * self.chunk, self.chunk)
        self.wide[pl.ds(at, self.chunk), :] = self.held[
            block, pl.ds(pl.multiple_of(c * self.chunk, self.chunk), self.chunk), :
        ].astype(F32)

    def own(self, c, value):
        at = pl.multiple_of(c * self.chunk, self.chunk)
        self.held[self.me, pl.ds(at, self.chunk), :] = value
        self.copy(0, c, self.me, self.far).start()
        self.copy(1, c, self.me, self.near).start()
        self.widen(self.me, c)

    def relay(self, c):
        self.copy(0, c, self.far, self.far).wait_recv()
        self.copy(2, c, self.far, self.near).start()
        self.widen(self.far, c)
        self.copy(1, c, self.near, self.near).wait_recv()
        self.widen(self.near, c)

    def arrive(self, c):
        self.copy(2, c, self.last, self.near).wait_recv()
        self.widen(self.last, c)

    def inside(self, b):
        @pl.when(b >= LAG)
        def _():
            self.relay(b - LAG)

        @pl.when(b >= LAG + 1)
        def _():
            self.arrive(b - LAG - 1)

    def finish(self, count):
        def tail(c, carry):
            self.relay(c)

            @pl.when(c >= 1)
            def _():
                self.arrive(c - 1)

            return carry

        lax.fori_loop(max(count - LAG, 0), count, tail, 0)
        self.arrive(count - 1)

        def end(c, carry):
            self.copy(0, c, self.me, self.far).wait_send()
            self.copy(1, c, self.me, self.near).wait_send()
            self.copy(2, c, self.far, self.near).wait_send()
            return carry

        lax.fori_loop(0, count, end, 0)


LAG = 2
COL_LAG = 3


def layer_one_kernel(
    col_size, points_hbm, slots_hbm, w_in_hbm, w_out_hbm, gate_up_hbm, down_hbm, out, wide,
    inverse, route, held, slot_all, points, w_in, w_out, gate_up, down, loaded, send, recv,
    s_send, s_recv,
):
    rows = points.shape[0]
    count = rows // BALL
    me, near, far = row_peers()
    other = far + near - me
    loads = [
        pltpu.make_async_copy(source, target, loaded.at[i])
        for i, (source, target) in enumerate(
            (
                (slots_hbm, slot_all.at[me]),
                (points_hbm, points),
                (w_in_hbm.at[0], w_in),
                (w_out_hbm.at[0], w_out),
                (gate_up_hbm.at[0], gate_up),
                (down_hbm.at[0], down),
            )
        )
    ]
    for load in loads:
        load.start()
    greet((near, far, other), "row")
    loads[0].wait()

    def slot_copy(kind, block, peer):
        return pltpu.make_async_remote_copy(
            src_ref=slot_all.at[me],
            dst_ref=slot_all.at[block],
            send_sem=s_send.at[kind],
            recv_sem=s_recv.at[kind],
            device_id={"row": peer},
            device_id_type=pl.DeviceIdType.MESH,
        )

    for kind, peer in enumerate((near, far, other)):
        slot_copy(kind, me, peer).start()
    slots = slot_all[me]
    route[...] = slots // (rows * col_size) * rows + slots % rows
    for load in loads[1:]:
        load.wait()
    gather = RowGather(held, wide, BALL, send, recv)

    def step(b, carry):
        u = points[pl.ds(b * BALL, BALL), :]
        mixed = (u.astype(F32) + fine_attention(u, w_in[...], w_out[...])).astype(BF16)
        value = ff_sum(mixed, gate_up[...], down[...]).astype(BF16)
        out[pl.ds(pl.multiple_of(b * BALL, BALL), BALL), :] = value
        gather.own(b, value)
        gather.inside(b)
        return carry

    lax.fori_loop(0, count, step, 0)
    for kind, peer in enumerate((near, far, other)):
        slot_copy(kind, peer, peer).wait()
    lines, lanes = slot_all.shape[1:]
    row_id = lax.broadcasted_iota(jnp.int32, (lines, lanes), 0)
    lane_id = lax.broadcasted_iota(jnp.int32, (lines, lanes), 1).astype(F32)
    sub_id = lax.broadcasted_iota(jnp.int32, (lanes, lanes), 0)
    left, right = [], []
    for r in range(slot_all.shape[0]):
        for c in range(lines):
            line = slot_all[r, c:c + 1, :]
            line = jnp.where(line // (rows * col_size) == me, line % rows, rows)
            hit = row_id == line // lanes
            left.append(
                jnp.concatenate(
                    (jnp.where(hit, float(r * lines + c), 0.0), jnp.where(hit, lane_id, 0.0)),
                    axis=0,
                ).astype(BF16)
            )
            right.append(jnp.where(sub_id == line % lanes, 1.0, 0.0).astype(BF16))
    found = dot_t(jnp.concatenate(left, axis=1), jnp.concatenate(right, axis=1))
    inverse[...] = (found[:lines] * lanes + found[lines:]).astype(jnp.int32)

    gather.finish(count)


def take_rows(wide, index, base, taken):
    unit = 32

    def step(i, carry):
        for j in range(unit):
            at = i * unit + j
            taken[pl.ds(at, 1), :] = wide[pl.ds(index[base + at], 1), :]
        return carry

    lax.fori_loop(0, taken.shape[0] // unit, step, 0)


def turn_kernel(source, index, w_in, w_out, wide, held, taken, send, recv):
    rows = held.shape[1]
    count = rows // BALL
    me, near, far = row_peers()
    greet((near, far), "row")
    gather = RowGather(held, wide, BALL, send, recv)

    def step(b, carry):
        take_rows(source, index, b * BALL, taken)
        u = taken[...].astype(BF16)
        gather.own(b, fine_attention(u, w_in[1], w_out[1]).astype(BF16))
        gather.inside(b)
        return carry

    lax.fori_loop(0, count, step, 0)

    gather.finish(count)


def layer_two_kernel(
    first, wide, index, gate_up, down, pool, w_in, second, own, queries, keys, values, pooled,
    taken, tall, send, recv
):
    rows = second.shape[0]
    count = rows // BALL
    small = BALL // FAN
    col = lax.axis_index("col")
    me = col % GROUP
    base = col - me
    flip = me + 1 - 2 * (me % 2)
    peers = [(me + 2 * step) % GROUP for step in range(1, GROUP // 2)]
    greet([base + p for p in [flip] + peers], "col")
    pieces = recv.shape[1]
    piece = pooled.shape[1] // pieces
    per = count // pieces

    def copy(kind, c, block, peer):
        spot = pooled.at[block, pl.ds(c * piece, piece)]
        return pltpu.make_async_remote_copy(
            src_ref=spot,
            dst_ref=spot,
            send_sem=send.at[kind, c],
            recv_sem=recv.at[kind, c],
            device_id={"col": base + peer},
            device_id_type=pl.DeviceIdType.MESH,
        )

    lead = GROUP // 2

    def source_of(kind):
        return (me + GROUP - 2 * kind) % GROUP

    def step(c, carry):
        def ball(i, carry):
            b = c * per + i
            at = pl.multiple_of(b * BALL, BALL)
            take_rows(wide, index, b * BALL, taken)
            mixed = (
                first[pl.ds(at, BALL), :].astype(F32) + taken[...]
            ).astype(BF16)
            result = ff_sum(mixed, gate_up[1], down[1]).astype(BF16)
            second[pl.ds(at, BALL), :] = result
            for t in range(tall.shape[0]):
                tall[t, pl.ds(pl.multiple_of(i * BALL, BALL), BALL), :] = result[
                    :, t * LANES:(t + 1) * LANES
                ].astype(F32)
            return carry

        lax.fori_loop(0, per, ball, 0)
        side = [
            tall[t, pl.ds(j, piece, stride=FAN), :].astype(BF16)
            for j in range(FAN)
            for t in range(tall.shape[0])
        ]
        total = dot(jnp.concatenate(side, axis=1), pool[...])
        pooled[me, pl.ds(pl.multiple_of(c * piece, piece), piece), :] = total.astype(BF16)
        copy(0, c, me, flip).start()
        for kind in range(1, lead):
            copy(kind, c, me, peers[kind - 1]).start()

        @pl.when(c >= COL_LAG)
        def _():
            relay(c - COL_LAG, 0)

        return carry

    def relay(c, carry):
        for kind in range(1, lead):
            copy(kind, c, source_of(kind), peers[0]).wait_recv()
            copy(lead - 1 + kind, c, source_of(kind), flip).start()
        return carry

    lax.fori_loop(0, pieces, step, 0)
    width = pool.shape[1]
    block_rows = pooled.shape[1]
    half = block_rows // 2

    def project(block, at, size):
        packed = dot(normed(pooled[block, at:at + size, :]), w_in[:, width:]).astype(BF16)
        spot = pl.ds(pl.multiple_of(block * block_rows + at, size), size)
        keys[spot, :] = packed[:, :width]
        values[spot, :] = packed[:, width:]

    def arrived(kind, block):
        def one(c, carry):
            copy(kind, c, block, flip).wait_recv()
            return carry

        lax.fori_loop(0, pieces, one, 0)

    direct = [source_of(kind) for kind in range(1, lead)]
    own[...] = pooled[me]
    queries[...] = dot(normed(pooled[me]), w_in[:, :width]).astype(BF16)
    project(me, 0, block_rows)
    start = max(pieces - COL_LAG, 0)
    for c in range(start, pieces):
        relay(c, 0)
        if c == start:
            arrived(0, flip)
            project(flip, 0, block_rows)
        if c == start + 1:
            for block in direct:
                project(block, 0, half)
    for block in direct:
        project(block, half, half)
    for kind in range(1, lead):
        origin = source_of(kind)
        block = origin + 1 - 2 * (origin % 2)
        arrived(lead - 1 + kind, block)
        project(block, 0, block_rows)

    def end(c, carry):
        copy(0, c, me, flip).wait_send()
        for kind in range(1, lead):
            copy(kind, c, me, peers[kind - 1]).wait_send()
            copy(lead - 1 + kind, c, source_of(kind), flip).wait_send()
        return carry

    lax.fori_loop(0, pieces, end, 0)


def coarse_kernel(
    pooled, queries, keys, values, second, w_out, gate_up, down, unpool, out, lifted
):
    own = pooled[...]
    rows, width = own.shape
    size = width // CHEADS
    factor = size ** -0.5 * LOG2E
    q = queries[...]
    part = 256
    head_of = lax.broadcasted_iota(jnp.int32, (rows, part), 1) // size
    zero = jnp.zeros((), BF16)
    mixture = []
    for g in range(width // part):
        at = g * part
        acc = jnp.zeros((rows, part), F32)
        for h in range(part // size):
            mine = head_of == h
            s = dot_t(jnp.where(mine, q[:, at:at + part], zero), keys[:, at:at + part])
            m = jnp.max(s, axis=-1, keepdims=True)
            e = jnp.exp2((s - m) * factor)
            r = dot(e.astype(BF16), values[:, at:at + part])
            acc = jnp.where(mine, r / jnp.sum(e, axis=-1, keepdims=True), acc)
        mixture.append(acc.astype(BF16))
    mixed = (own.astype(F32) + dot(jnp.concatenate(mixture, axis=1), w_out[...])).astype(BF16)
    coarse = ff_sum(mixed, gate_up[...], down[...]).astype(BF16)
    up = normed(coarse)
    fine = out.shape[1]
    for j in range(FAN):
        part_up = dot(up, unpool[:, j * fine:(j + 1) * fine])
        for t in range(lifted.shape[0]):
            lifted[t, pl.ds(j, rows, stride=FAN), :] = part_up[:, t * LANES:(t + 1) * LANES]
    for c in range(out.shape[0] // BALL):
        at = c * BALL
        for t in range(lifted.shape[0]):
            lane = slice(t * LANES, (t + 1) * LANES)
            out[at:at + BALL, lane] = (
                second[at:at + BALL, lane].astype(F32) + lifted[t, at:at + BALL, :]
            ).astype(BF16)


VMEM = pl.BlockSpec(memory_space=pltpu.VMEM)
SMEM = pl.BlockSpec(memory_space=pltpu.SMEM)
DMA = pltpu.SemaphoreType.DMA


def local(
    points,
    rotated_slot,
    fine_attend_in,
    fine_attend_out,
    fine_gate_up,
    fine_down,
    pool_weight,
    coarse_attend_in,
    coarse_attend_out,
    coarse_gate_up,
    coarse_down,
    unpool_weight,
):
    rows, width = points.shape
    row_size = lax.axis_size("row")
    col_size = lax.axis_size("col")
    count = rows // BALL
    small = rows // FAN
    coarse_width = pool_weight.shape[1]
    lanes = LANES
    lines = rows // lanes
    mib = 1024 * 1024
    everyone = jax.ShapeDtypeStruct((row_size * rows, width), F32)
    held = pltpu.VMEM((row_size, rows, width), BF16)
    scalars = jax.ShapeDtypeStruct((lines, lanes), jnp.int32)

    first, wide, inverse, route = pl.pallas_call(
        functools.partial(layer_one_kernel, col_size),
        out_shape=(jax.ShapeDtypeStruct((rows, width), BF16), everyone, scalars, scalars),
        in_specs=[pl.BlockSpec(memory_space=pltpu.HBM)] * 6,
        out_specs=(VMEM,) * 4,
        scratch_shapes=[
            held,
            pltpu.VMEM((row_size, lines, lanes), jnp.int32),
            pltpu.VMEM(points.shape, BF16),
            pltpu.VMEM(fine_attend_in.shape[1:], BF16),
            pltpu.VMEM(fine_attend_out.shape[1:], BF16),
            pltpu.VMEM(fine_gate_up.shape[1:], BF16),
            pltpu.VMEM(fine_down.shape[1:], BF16),
            DMA((6,)),
            DMA((3, count)),
            DMA((3, count)),
            DMA((3,)),
            DMA((3,)),
        ],
        compiler_params=pltpu.CompilerParams(
            collective_id=0, has_side_effects=True, vmem_limit_bytes=36 * mib
        ),
        name="layer_one",
    )(
        *(
            pltpu.with_memory_space_constraint(array, pltpu.HBM)
            for array in (
                points,
                rotated_slot.reshape(lines, lanes),
                fine_attend_in,
                fine_attend_out,
                fine_gate_up,
                fine_down,
            )
        )
    )

    turned = pl.pallas_call(
        turn_kernel,
        out_shape=everyone,
        in_specs=[VMEM, SMEM, VMEM, VMEM],
        out_specs=VMEM,
        scratch_shapes=[
            held,
            pltpu.VMEM((BALL, width), F32),
            DMA((3, count)),
            DMA((3, count)),
        ],
        compiler_params=pltpu.CompilerParams(
            collective_id=1, has_side_effects=True, vmem_limit_bytes=24 * mib
        ),
        name="turn",
    )(wide, inverse.reshape(-1), fine_attend_in, fine_attend_out)

    pieces = count
    kinds = GROUP - 1
    one = jax.ShapeDtypeStruct((small, coarse_width), BF16)
    every = jax.ShapeDtypeStruct((GROUP * small, coarse_width), BF16)
    second, *coarse_parts = pl.pallas_call(
        layer_two_kernel,
        out_shape=(
            jax.ShapeDtypeStruct((rows, width), BF16),
            one,
            one,
            every,
            every,
        ),
        in_specs=[VMEM, VMEM, SMEM, VMEM, VMEM, VMEM, VMEM],
        out_specs=(VMEM,) * 5,
        scratch_shapes=[
            pltpu.VMEM((GROUP, small, coarse_width), BF16),
            pltpu.VMEM((BALL, width), F32),
            pltpu.VMEM((width // LANES, rows // pieces, LANES), F32),
            DMA((kinds, pieces)),
            DMA((kinds, pieces)),
        ],
        compiler_params=pltpu.CompilerParams(
            collective_id=2, has_side_effects=True, vmem_limit_bytes=20 * mib
        ),
        name="layer_two",
    )(first, turned, route.reshape(-1), fine_gate_up, fine_down, pool_weight, coarse_attend_in)

    return pl.pallas_call(
        coarse_kernel,
        out_shape=jax.ShapeDtypeStruct((rows, width), BF16),
        in_specs=[VMEM] * 9,
        out_specs=VMEM,
        scratch_shapes=[
            pltpu.VMEM((width // LANES, rows, LANES), F32),
        ],
        compiler_params=pltpu.CompilerParams(vmem_limit_bytes=22 * mib),
        name="coarse",
    )(
        *coarse_parts,
        second,
        coarse_attend_out,
        coarse_gate_up,
        coarse_down,
        unpool_weight,
    )


def solution(mesh):
    split = P(("row", "col"), None)
    placed = (split, P(("row", "col"))) + (P(),) * 10
    return jax.shard_map(local, mesh=mesh, in_specs=placed, out_specs=split, check_vma=False)
```
